32 devices in a mesh: tm: 4 (over y, x), tile: 8 (over z, core).
Axes of the slice: x: 2, y: 2, z: 4, core: 2. Of those that a mesh axis runs over, the one named last changes fastest.
Arguments:
- diag_blocks: float32 [16384, 4096], P(('tm', 'tile')), as said below
- coupling: float32 [16384, 4096], P(('tm', 'tile')), as said below
- next_diag: float32 [16384, 4096], P(('tm', 'tile')), as said below
- arrow_now: float32 [128, 4096], P('tm'), may hold values from -0.4375 to 0.4375
- arrow_next: float32 [128, 4096], P('tm'), may hold values from -0.4375 to 0.4375
- arrow_tip: float32 [128, 32], P('tm'), may hold values from -6 to 6
Outputs:
- factor_lower: float32 [16384, 4096], P(('tm', 'tile'))
- coupling_out: float32 [16384, 4096], P(('tm', 'tile'))
- arrow_factor: float32 [128, 4096], P('tm')
- handed_diag: float32 [16384, 4096], P(('tm', 'tile'))
- handed_arrow: float32 [128, 4096], P('tm')
- handed_tip: float32 [128, 32], P('tm')
The draws below stay inside these ranges and needn't reach their ends.
Inputs may be any that keep to these rules, and one draw needn't show every extreme that they name: `diag_blocks`: each 4096 x 4096 block is symmetric positive definite. `next_diag`: each 4096 x 4096 block is symmetric positive definite. `coupling`: with the diag_blocks block and the next_diag block of its time step, each 4096 x 4096 block forms a symmetric positive definite two-block precision matrix.
All inputs are finite; a program needn't handle non-finite values.
Results may differ from the reference program's by a relative error of at most 0.0001.
Values sent between devices are 32-bit elements; how exact they have to be, the bound alone decides.
No kernel may reach another device: no remote copies, remote signals or barrier semaphores. Data moves between devices by JAX's collectives and lax.ppermute only.
A program may use at most 256 MiB of HBM per device.

```python
import math
import jax
import jax.numpy as jnp
from jax import lax

N = 4096
ARROW = 32
PANEL = 512
PANELS = 2
STEPS = 4


def spd_block(key, ridge_lo, ridge_hi):
    key_noise = jax.random.fold_in(key, 1)
    key_ridge = jax.random.fold_in(key, 2)
    key_scale = jax.random.fold_in(key, 3)
    key_place = jax.random.fold_in(key, 4)
    raw_draw = jax.random.normal(key_noise, (N, N), jnp.float32)
    ridge = jax.random.uniform(key_ridge, (N,), jnp.float32, ridge_lo, ridge_hi)
    scales = jax.random.uniform(key_scale, (N,), jnp.float32, 0.4, 0.8)
    noise = (raw_draw + raw_draw.T) * (0.35355339 / math.sqrt(N))
    places = lax.iota(jnp.float32, N) + jax.random.uniform(key_place, (N,), jnp.float32, -0.45, 0.45)
    reach = max(1.0, N / 128.0)
    kernel = scales[:, None] * scales[None, :] * jnp.exp(-jnp.abs(places[:, None] - places[None, :]) / reach)
    identity = jnp.eye(N, dtype=jnp.float32)
    return noise + kernel + identity * ridge[:, None]


def step_blocks(key, step_t):
    base = jax.random.fold_in(jax.random.fold_in(key, 101), step_t)
    block_a = spd_block(jax.random.fold_in(base, 1), 1.4, 2.4)
    key_rho = jax.random.fold_in(base, 2)
    key_extra = jax.random.fold_in(base, 3)
    rho = jax.random.uniform(key_rho, (), jnp.float32, 0.55, 0.8)
    extra = jax.random.normal(key_extra, (N, N), jnp.float32)
    block_c = -rho * block_a + extra * (0.15 / math.sqrt(N))
    block_d = rho * rho * block_a + spd_block(jax.random.fold_in(base, 4), 2.0, 3.0)
    return (block_a, block_c, block_d)


def stacked(key, which):
    blocks = lax.map(lambda step_t: step_blocks(key, step_t)[which], jnp.arange(STEPS, dtype=jnp.int32))
    return blocks.reshape(STEPS * N, N)


def draw_diag_blocks(key, part):
    return stacked(key, 0)


def draw_coupling(key, part):
    return stacked(key, 1)


def draw_next_diag(key, part):
    return stacked(key, 2)


def block_levels(stream_key, extent, cuts, smallest, top_value):
    def one(axis_at, shards_of):
        heights = jax.random.uniform(jax.random.fold_in(jax.random.fold_in(stream_key, 6), axis_at), (shards_of,), jnp.float32, smallest / len(cuts), top_value / len(cuts))
        return jnp.repeat(jnp.exp(heights), extent[axis_at] // shards_of).reshape((-1,) + (1,) * (len(extent) - axis_at - 1))

    gain = one(*cuts[0])
    for cut in cuts[1:]:
        gain = gain * one(*cut)
    return gain


def scatter_about(own_key, dims, width, limit, shards=(), held_as=jnp.bfloat16):
    array = jax.random.normal(own_key, dims, jnp.float32) * width
    if len(shards) > 0:
        array = block_levels(own_key, dims, shards, -0.22, 0.18) * array
    return jnp.clip(array, min=-limit, max=limit).astype(held_as)


def setup_inputs(seed: int = 0) -> dict:
    keys = jax.random.split(jax.random.key(seed), 7)
    return {
        "diag_blocks": draw_diag_blocks(jax.random.fold_in(keys[6], 71), 0),
        "coupling": draw_coupling(jax.random.fold_in(keys[6], 71), 0),
        "next_diag": draw_next_diag(jax.random.fold_in(keys[6], 71), 0),
        "arrow_now": scatter_about(keys[3], (STEPS * ARROW, N), (N // 24) ** -0.5, 0.4375, ((0, 4),), jnp.float32),
        "arrow_next": scatter_about(keys[4], (STEPS * ARROW, N), (N // 24) ** -0.5, 0.4375, ((0, 4),), jnp.float32),
        "arrow_tip": scatter_about(keys[5], (STEPS * ARROW, ARROW), 1.0, 6.0, ((0, 4),), jnp.float32),
    }


precise = lax.Precision.HIGHEST

def outer_rows(left_rows, right_rows):
    return lax.dot_general(left_rows.astype(jnp.float32), right_rows.astype(jnp.float32), (((1,), (1,)), ((), ())), precision=precise, preferred_element_type=jnp.float32)

def solve_rows(factor, block):
    return jax.scipy.linalg.solve_triangular(factor, block.T, lower=True).T

def block_step(work_a, work_c, next_d, arrow_a, arrow_b, tip_block):
    row_ids = jnp.arange(N, dtype=jnp.int32)
    for number in range(PANELS):
        offset = number * PANEL
        ending = offset + PANEL
        factor = jnp.linalg.cholesky(work_a[offset:ending, offset:ending])
        panel_a = jnp.where((row_ids >= offset)[:, None], solve_rows(factor, work_a[:, offset:ending]), 0.0)
        panel_c = solve_rows(factor, work_c[:, offset:ending])
        panel_r = solve_rows(factor, arrow_a[:, offset:ending])
        work_a = work_a.at[:, offset:ending].set(panel_a)
        work_c = work_c.at[:, offset:ending].set(panel_c)
        arrow_a = arrow_a.at[:, offset:ending].set(panel_r)
        keep_rows = (row_ids >= ending)[:, None]
        targets = panel_a[ending:]
        work_a = work_a.at[:, ending:].add(-jnp.where(keep_rows, outer_rows(panel_a, targets), 0.0))
        work_c = work_c.at[:, ending:].add(-outer_rows(panel_c, targets))
        arrow_a = arrow_a.at[:, ending:].add(-outer_rows(panel_r, targets))
        next_d = next_d - outer_rows(panel_c, panel_c)
        arrow_b = arrow_b - outer_rows(panel_r, panel_c)
        tip_block = tip_block - outer_rows(panel_r, panel_r)
    col_ids = jnp.arange(N, dtype=jnp.int32)
    lower_part = jnp.where(col_ids[None, :] <= row_ids[:, None], work_a, 0.0)
    return (lower_part, work_c, arrow_a, next_d, arrow_b, tip_block)

def reference(diag_blocks, coupling, next_diag, arrow_now, arrow_next, arrow_tip):
    factors, couplings, arrows, nexts, arrow_nexts, tips = ([], [], [], [], [], [])
    for step_t in range(STEPS):
        rows_a = slice(step_t * N, (step_t + 1) * N)
        rows_r = slice(step_t * ARROW, (step_t + 1) * ARROW)
        result = block_step(diag_blocks[rows_a], coupling[rows_a], next_diag[rows_a], arrow_now[rows_r], arrow_next[rows_r], arrow_tip[rows_r])
        factors.append(result[0])
        couplings.append(result[1])
        arrows.append(result[2])
        nexts.append(result[3])
        arrow_nexts.append(result[4])
        tips.append(result[5])
    handed_diag = jnp.concatenate([jnp.zeros((N, N), jnp.float32)] + nexts[:-1], axis=0)
    handed_arrow = jnp.concatenate([jnp.zeros((ARROW, N), jnp.float32)] + arrow_nexts[:-1], axis=0)
    handed_tip = jnp.concatenate([jnp.zeros((ARROW, ARROW), jnp.float32)] + tips[:-1], axis=0)
    return (jnp.concatenate(factors, axis=0), jnp.concatenate(couplings, axis=0), jnp.concatenate(arrows, axis=0), handed_diag, handed_arrow, handed_tip)
```

```python
import jax
import jax.numpy as jnp
from jax import lax
from jax.experimental import pallas as pl
from jax.experimental.pallas import tpu as pltpu
from jax.sharding import PartitionSpec as P

BLK = 128
precise = lax.Precision.HIGHEST


def dot_nt(a, b):
    return lax.dot_general(a, b, (((1,), (1,)), ((), ())), precision=precise, preferred_element_type=jnp.float32)


def dot_nn(a, b):
    return lax.dot_general(a, b, (((1,), (0,)), ((), ())), precision=precise, preferred_element_type=jnp.float32)


def spread_lane(tile, lane):
    return jnp.broadcast_to(tile[:, lane:lane + 1], (8, BLK))


def spread_row(tile, row):
    return jnp.broadcast_to(tile[row:row + 1, :], (8, BLK))


def diag_inverse(block_ref, inverse_ref):
    groups = BLK // 8
    sub = lax.broadcasted_iota(jnp.int32, (8, BLK), 0)
    lane = lax.broadcasted_iota(jnp.int32, (8, BLK), 1)
    left = [block_ref[8 * g:8 * g + 8, :] for g in range(groups)]
    right = [jnp.where(lane == sub + 8 * g, 1.0, 0.0).astype(jnp.float32) for g in range(groups)]
    for g in range(groups):
        rows, unit = left[g], right[g]
        cols = [spread_lane(rows, 8 * g + c) for c in range(8)]
        scale = jnp.zeros((8, BLK), jnp.float32)
        kept = []
        for k in range(8):
            pivot = spread_row(cols[k], k)
            inv = 1.0 / pivot
            scale = jnp.where(sub == k, lax.rsqrt(pivot), scale)
            row_l, row_r = spread_row(rows, k), spread_row(unit, k)
            heads = {c: spread_row(cols[c], k) for c in range(k + 1, 8)}
            kept.append((inv, row_l, row_r, heads))
            if k < 7:
                f = jnp.where(sub > k, cols[k] * inv, 0.0)
                for c in range(k + 1, 8):
                    cols[c] = cols[c] - f * heads[c]
                rows = rows - f * row_l
                unit = unit - f * row_r
        inverse_ref[8 * g:8 * g + 8, :] = unit * scale
        for r in range(g + 1, groups):
            fac = [spread_lane(left[r], 8 * g + c) for c in range(8)]
            lo, ro = left[r], right[r]
            for k in range(8):
                inv, row_l, row_r, heads = kept[k]
                f = fac[k] * inv
                for c in range(k + 1, 8):
                    fac[c] = fac[c] - f * heads[c]
                lo = lo - f * row_l
                ro = ro - f * row_r
            left[r], right[r] = lo, ro


def chain_kernel(k_ref, out_ref, l_ref, s_ref, g_ref, d_ref, m_ref):
    n = k_ref.shape[0]
    nb = n // BLK
    out_ref[...] = jnp.zeros((n, n), jnp.float32)

    def step(k, carry):
        for i in range(nb):
            @pl.when(k == i)
            def _(i=i):
                at, to = i * BLK, (i + 1) * BLK
                s = k_ref[at:, at:to]
                if i:
                    s = s - dot_nt(l_ref[at:, :at], l_ref[at:to, :at])
                    g_ref[:, :at] = dot_nn(l_ref[at:to, :at], out_ref[:at, :at])
                s_ref[at:, :] = s
                d_ref[...] = s[:BLK]

        diag_inverse(d_ref, m_ref)
        for i in range(nb):
            @pl.when(k == i)
            def _(i=i):
                at, to = i * BLK, (i + 1) * BLK
                m = m_ref[...]
                if i < nb - 1:
                    l_ref[to:, at:to] = dot_nt(s_ref[to:, :], m)
                out_ref[at:to, at:to] = m
                if i:
                    out_ref[at:to, :at] = -dot_nn(m, g_ref[:, :at])
        return carry

    lax.fori_loop(0, nb, step, 0)


def chain(k):
    n = k.shape[0]
    return pl.pallas_call(
        chain_kernel,
        out_shape=jax.ShapeDtypeStruct((n, n), jnp.float32),
        in_specs=[pl.BlockSpec(memory_space=pltpu.VMEM)],
        out_specs=pl.BlockSpec(memory_space=pltpu.VMEM),
        scratch_shapes=[pltpu.VMEM((n, n), jnp.float32), pltpu.VMEM((n, BLK), jnp.float32),
                        pltpu.VMEM((BLK, n), jnp.float32), pltpu.VMEM((BLK, BLK), jnp.float32),
                        pltpu.VMEM((BLK, BLK), jnp.float32)],
        compiler_params=pltpu.CompilerParams(vmem_limit_bytes=40 << 20),
        cost_estimate=pl.CostEstimate(flops=60_000_000_000, bytes_accessed=8 << 20, transcendentals=0),
    )(k)


def nt(left, right):
    return lax.dot_general(left, right, (((1,), (1,)), ((), ())), precision=lax.Precision.HIGH, preferred_element_type=jnp.float32)


def nn(left, right):
    return lax.dot_general(left, right, (((1,), (0,)), ((), ())), precision=lax.Precision.HIGH, preferred_element_type=jnp.float32)


def handed(value):
    count = lax.axis_size("tm")
    return lax.ppermute(value, "tm", [(t, t + 1) for t in range(count - 1)])


def gather_rows(own):
    return lax.all_gather(own, "tile", axis=0, tiled=True)


def local(diag_blocks, coupling, next_diag, arrow_now, arrow_next, arrow_tip):
    rows, cols = diag_blocks.shape
    pivots = cols // 4
    arrows = arrow_now.shape[0]
    panel_a, panel_c, panel_r = diag_blocks[:, :pivots], coupling[:, :pivots], arrow_now[:, :pivots]
    cut = rows * 3 // 4
    past_c = handed(panel_c)
    past_d = [handed(next_diag[:cut]), handed(next_diag[cut:])]
    past_b = handed(arrow_next)
    all_a = gather_rows(panel_a)
    inverse = chain(all_a[:pivots])
    solved = nt(jnp.concatenate([panel_a, panel_c, panel_r]), inverse)
    weight = nn(solved, inverse)
    past_w = handed(weight[rows:])
    past_tip = handed(arrow_tip - nt(solved[2 * rows:], solved[2 * rows:]))
    rest = nt(weight, all_a[pivots:])
    row_ids = lax.axis_index("tile") * rows + lax.iota(jnp.int32, rows)
    keep = lax.iota(jnp.int32, cols)[None, :] <= row_ids[:, None]
    factor = jnp.concatenate([solved[:rows], diag_blocks[:, pivots:] - rest[:rows]], axis=1)
    factor = jnp.where(keep, factor, 0.0)
    coupled = jnp.concatenate([solved[rows:2 * rows], coupling[:, pivots:] - rest[rows:2 * rows]], axis=1)
    arrow = jnp.concatenate([solved[2 * rows:], arrow_now[:, pivots:] - rest[2 * rows:]], axis=1)
    all_c = gather_rows(past_c)
    past_d = jnp.concatenate([past_d[0] - nt(past_w[:cut], all_c), past_d[1] - nt(past_w[cut:rows], all_c)])
    past_b = past_b - nt(past_w[rows:], all_c)
    return (factor, coupled, arrow, past_d, past_b, past_tip)


def solution(mesh):
    split, whole = P(("tm", "tile"), None), P("tm", None)
    return jax.shard_map(
        local,
        mesh=mesh,
        in_specs=(split, split, split, whole, whole, whole),
        out_specs=(split, split, whole, split, whole, whole),
        check_vma=False,
    )
```

```python
import functools

import jax
import jax.numpy as jnp
from jax import lax
from jax.experimental import pallas as pl
from jax.experimental.pallas import tpu as pltpu
from jax.sharding import PartitionSpec as P

BLK = 128
precise = lax.Precision.HIGHEST


def dot_nt(a, b):
    return lax.dot_general(a, b, (((1,), (1,)), ((), ())), precision=precise, preferred_element_type=jnp.float32)


def dot_nn(a, b):
    return lax.dot_general(a, b, (((1,), (0,)), ((), ())), precision=precise, preferred_element_type=jnp.float32)


def spread_lane(tile, lane):
    return jnp.broadcast_to(tile[:, lane:lane + 1], (8, BLK))


def spread_row(tile, row):
    return jnp.broadcast_to(tile[row:row + 1, :], (8, BLK))


def diag_inverse(block_ref, inverse_ref):
    groups = BLK // 8
    sub = lax.broadcasted_iota(jnp.int32, (8, BLK), 0)
    lane = lax.broadcasted_iota(jnp.int32, (8, BLK), 1)
    left = [block_ref[8 * g:8 * g + 8, :] for g in range(groups)]
    right = [jnp.where(lane == sub + 8 * g, 1.0, 0.0).astype(jnp.float32) for g in range(groups)]
    for g in range(groups):
        rows, unit = left[g], right[g]
        cols = [spread_lane(rows, 8 * g + c) for c in range(8)]
        scale = jnp.zeros((8, BLK), jnp.float32)
        kept = []
        for k in range(8):
            pivot = spread_row(cols[k], k)
            inv = 1.0 / pivot
            scale = jnp.where(sub == k, lax.rsqrt(pivot), scale)
            row_l, row_r = spread_row(rows, k), spread_row(unit, k)
            heads = {c: spread_row(cols[c], k) for c in range(k + 1, 8)}
            kept.append((inv, row_l, row_r, heads))
            if k < 7:
                f = jnp.where(sub > k, cols[k] * inv, 0.0)
                for c in range(k + 1, 8):
                    cols[c] = cols[c] - f * heads[c]
                rows = rows - f * row_l
                unit = unit - f * row_r
        inverse_ref[8 * g:8 * g + 8, :] = unit * scale
        for r in range(g + 1, groups):
            fac = [spread_lane(left[r], 8 * g + c) for c in range(8)]
            lo, ro = left[r], right[r]
            for k in range(8):
                inv, row_l, row_r, heads = kept[k]
                f = fac[k] * inv
                for c in range(k + 1, 8):
                    fac[c] = fac[c] - f * heads[c]
                lo = lo - f * row_l
                ro = ro - f * row_r
            left[r], right[r] = lo, ro


def chain_kernel(k_ref, out_ref, l_ref, s_ref, g_ref, d_ref, m_ref):
    n = k_ref.shape[0]
    nb = n // BLK
    out_ref[...] = jnp.zeros((n, n), jnp.float32)

    def step(k, carry):
        for i in range(nb):
            @pl.when(k == i)
            def _(i=i):
                at, to = i * BLK, (i + 1) * BLK
                s = k_ref[at:, at:to]
                if i:
                    s = s - dot_nt(l_ref[at:, :at], l_ref[at:to, :at])
                    g_ref[:, :at] = dot_nn(l_ref[at:to, :at], out_ref[:at, :at])
                s_ref[at:, :] = s
                d_ref[...] = s[:BLK]

        diag_inverse(d_ref, m_ref)
        for i in range(nb):
            @pl.when(k == i)
            def _(i=i):
                at, to = i * BLK, (i + 1) * BLK
                m = m_ref[...]
                if i < nb - 1:
                    l_ref[to:, at:to] = dot_nt(s_ref[to:, :], m)
                out_ref[at:to, at:to] = m
                if i:
                    out_ref[at:to, :at] = -dot_nn(m, g_ref[:, :at])
        return carry

    lax.fori_loop(0, nb, step, 0)


def chain(k):
    n = k.shape[0]
    return pl.pallas_call(
        chain_kernel,
        out_shape=jax.ShapeDtypeStruct((n, n), jnp.float32),
        in_specs=[pl.BlockSpec(memory_space=pltpu.VMEM)],
        out_specs=pl.BlockSpec(memory_space=pltpu.VMEM),
        scratch_shapes=[pltpu.VMEM((n, n), jnp.float32), pltpu.VMEM((n, BLK), jnp.float32),
                        pltpu.VMEM((BLK, n), jnp.float32), pltpu.VMEM((BLK, BLK), jnp.float32),
                        pltpu.VMEM((BLK, BLK), jnp.float32)],
        compiler_params=pltpu.CompilerParams(vmem_limit_bytes=40 << 20),
        cost_estimate=pl.CostEstimate(flops=1_000_000, bytes_accessed=1 << 16, transcendentals=0),
    )(k)


def chain_picked_kernel(at_ref, *refs):
    pairs, (out_ref, k_ref, l_ref, s_ref, g_ref, d_ref, m_ref) = refs[:6], refs[6:]
    rows = k_ref.shape[0] // 2
    for which in range(3):
        for core in range(2):
            @pl.when((at_ref[0] == which) & (at_ref[1] == core))
            def _(which=which, core=core):
                pltpu.sync_copy(pairs[2 * which], k_ref.at[core * rows:(core + 1) * rows])
                pltpu.sync_copy(pairs[2 * which + 1], k_ref.at[(1 - core) * rows:(2 - core) * rows])
    chain_kernel(k_ref, out_ref, l_ref, s_ref, g_ref, d_ref, m_ref)


def chain_picked(at, pairs):
    n = 2 * pairs[0].shape[0]
    return pl.pallas_call(
        chain_picked_kernel,
        out_shape=jax.ShapeDtypeStruct((n, n), jnp.float32),
        grid_spec=pltpu.PrefetchScalarGridSpec(
            num_scalar_prefetch=1,
            grid=(1,),
            in_specs=[pl.BlockSpec(memory_space=pl.ANY)] * 6,
            out_specs=pl.BlockSpec((n, n), lambda i, at: (0, 0)),
            scratch_shapes=[pltpu.VMEM((n, n), jnp.float32), pltpu.VMEM((n, n), jnp.float32), pltpu.VMEM((n, BLK), jnp.float32),
                            pltpu.VMEM((BLK, n), jnp.float32), pltpu.VMEM((BLK, BLK), jnp.float32),
                            pltpu.VMEM((BLK, BLK), jnp.float32)],
        ),
        compiler_params=pltpu.CompilerParams(vmem_limit_bytes=40 << 20),
        cost_estimate=pl.CostEstimate(flops=1_000_000, bytes_accessed=1 << 16, transcendentals=0),
    )(at, *pairs)


def halves(x):
    high = x.astype(jnp.bfloat16)
    return high, (x - high.astype(jnp.float32)).astype(jnp.bfloat16)


def product(weights, other):
    (high, low), (other_high, other_low) = weights, other
    dims = (((1,), (1,)), ((), ()))
    total = lax.dot_general(high, other_high, dims, preferred_element_type=jnp.float32)
    total += lax.dot_general(high, other_low, dims, preferred_element_type=jnp.float32)
    return total + lax.dot_general(low, other_high, dims, preferred_element_type=jnp.float32)


LIGHT = pl.CostEstimate(flops=1_000_000, bytes_accessed=1 << 16, transcendentals=0)


def fetch(step, sources, buffer_ref, sems):
    for i in range(len(sources)):
        @pl.when(step == i)
        def _(i=i):
            copies = [pltpu.make_async_copy(sources[j], buffer_ref.at[j % 2], sems.at[j % 2])
                      for j in (i, i + 1) if j < len(sources)]
            if i == 0:
                copies[0].start()
            if len(copies) > 1:
                copies[1].start()
            copies[0].wait()


def panel_update_kernel(count, at_ref, high_ref, low_ref, solved_ref, a_ref, c_ref, r_ref, *rest):
    a_out, c_out, r_out, buffer_ref, sems = rest[-5:]
    step = pl.program_id(0)
    rows = a_ref.shape[0]
    fetch(step, rest[:count], buffer_ref, sems)
    block = at_ref[step]
    keep = (block * rows + lax.broadcasted_iota(jnp.int32, (rows, rows), 1)
            <= at_ref[count] + lax.broadcasted_iota(jnp.int32, (rows, rows), 0))
    solved = block * rows < high_ref.shape[1]

    @pl.when(solved)
    def _():
        a_out[...] = jnp.where(keep, solved_ref[:rows], 0.0)
        c_out[...] = solved_ref[rows:2 * rows]
        r_out[...] = solved_ref[2 * rows:]

    @pl.when(jnp.logical_not(solved))
    def _():
        x = halves(buffer_ref[step % 2])
        a_out[...] = jnp.where(keep, a_ref[...] - product((high_ref[:rows], low_ref[:rows]), x), 0.0)
        c_out[...] = c_ref[...] - product((high_ref[rows:2 * rows], low_ref[rows:2 * rows]), x)
        r_out[...] = r_ref[...] - product((high_ref[2 * rows:], low_ref[2 * rows:]), x)


def panel_update(at, weights, solved, bases, blocks, before):
    rows, arrows, pivots = bases[0].shape[0], bases[2].shape[0], solved.shape[1]
    last = pivots // rows - 1
    count = len(blocks)
    whole = pl.BlockSpec(memory_space=pl.ANY)
    fixed = pl.BlockSpec((2 * rows + arrows, pivots), lambda i, at: (0, 0))
    moving = [pl.BlockSpec((h, rows), lambda i, at: (0, at[i])) for h in (rows, rows, arrows)]
    in_specs = [fixed] * 2 + [pl.BlockSpec((2 * rows + arrows, rows), lambda i, at: (0, jnp.minimum(at[i], last)))]
    in_specs += moving + [whole] * count
    args = [at, *weights, solved, *bases, *blocks]
    aliases = {}
    if before is not None:
        aliases = {len(args) + i: i for i in range(3)}
        in_specs += [whole] * 3
        args += list(before)
    return pl.pallas_call(
        functools.partial(panel_update_kernel, count),
        out_shape=[jax.ShapeDtypeStruct(b.shape, b.dtype) for b in bases],
        grid_spec=pltpu.PrefetchScalarGridSpec(
            num_scalar_prefetch=1, grid=(count,), in_specs=in_specs,
            out_specs=moving,
            scratch_shapes=[pltpu.VMEM((2, rows, pivots), jnp.float32), pltpu.SemaphoreType.DMA((2,))]),
        input_output_aliases=aliases,
        compiler_params=pltpu.CompilerParams(vmem_limit_bytes=48 << 20),
        cost_estimate=LIGHT,
    )(*args)


def schur_update_kernel(count, parts, arrow, at_ref, high_ref, low_ref, *rest):
    bases, sources, (*outs, buffer_ref, sems) = rest[:parts], rest[parts:parts + count], rest[-2 - (2 if arrow else 1):]
    step = pl.program_id(0)
    height, rows = outs[0].shape
    fetch(step, sources, buffer_ref, sems)
    x_ref = buffer_ref.at[step % 2]
    x = halves(x_ref[:rows])
    total = product((high_ref[:height], low_ref[:height]), x)
    start = 0
    for base in bases:
        end = start + base.shape[0]
        outs[0][start:end] = base[...] - total[start:end]
        start = end
    if arrow:
        base = jnp.concatenate([x_ref[rows:, :rows], x_ref[rows:, rows:2 * rows]], axis=0)
        outs[1][...] = base - product((high_ref[rows:], low_ref[rows:]), x)


def schur_update(at, weights, bases, blocks, before, row_at=0, arrow=True):
    rows, pivots = blocks[0].shape[0] - 16, blocks[0].shape[1]
    arrows, cols = weights[0].shape[0] - rows, bases[0].shape[1]
    height = sum(base.shape[0] for base in bases)
    count = len(blocks)
    whole = pl.BlockSpec(memory_space=pl.ANY)
    fixed = pl.BlockSpec((rows + arrows if arrow else height, pivots), lambda i, at: (row_at, 0))
    in_specs = [fixed] * 2 + [pl.BlockSpec((base.shape[0], rows), lambda i, at: (0, at[i])) for base in bases]
    in_specs += [whole] * count
    args = [at, *weights, *bases, *blocks]
    out_shape = [jax.ShapeDtypeStruct((rows, cols), jnp.float32)]
    out_specs = [pl.BlockSpec((height, rows), lambda i, at: (row_at, at[i]))]
    if arrow:
        out_shape.append(jax.ShapeDtypeStruct((arrows, cols), jnp.float32))
        out_specs.append(pl.BlockSpec((arrows, rows), lambda i, at: (0, at[i])))
    aliases = {}
    if before is not None:
        aliases = {len(args) + i: i for i in range(len(before))}
        in_specs += [whole] * len(before)
        args += list(before)
    return pl.pallas_call(
        functools.partial(schur_update_kernel, count, len(bases), arrow),
        out_shape=out_shape,
        grid_spec=pltpu.PrefetchScalarGridSpec(
            num_scalar_prefetch=1, grid=(count,), in_specs=in_specs, out_specs=out_specs,
            scratch_shapes=[pltpu.VMEM((2, rows + 16, pivots), jnp.float32), pltpu.SemaphoreType.DMA((2,))]),
        input_output_aliases=aliases,
        compiler_params=pltpu.CompilerParams(vmem_limit_bytes=48 << 20),
        cost_estimate=LIGHT,
    )(*args)


def nt(left, right):
    return lax.dot_general(left, right, (((1,), (1,)), ((), ())), precision=lax.Precision.HIGH, preferred_element_type=jnp.float32)


def nn(left, right):
    return lax.dot_general(left, right, (((1,), (0,)), ((), ())), precision=lax.Precision.HIGH, preferred_element_type=jnp.float32)


def handed(value):
    count = lax.axis_size("tm")
    return lax.ppermute(value, "tm", [(t, t + 1) for t in range(count - 1)])


def after(value, *others):
    return lax.optimization_barrier((value,) + others)[0]


def stage(values, *others):
    return lax.optimization_barrier(tuple(values) + others)[:len(values)]


def hop(value, pairs):
    return lax.ppermute(value, "tile", [(2 * a + c, 2 * b + c) for a, b in pairs for c in range(2)])


def sibling(value):
    return lax.ppermute(value, "tile", [(i, i ^ 1) for i in range(8)])


def bf16_halves(x):
    high = lax.reduce_precision(x, 8, 7)
    return high.astype(jnp.bfloat16), (x - high).astype(jnp.bfloat16)


def local_line(diag_blocks, coupling, next_diag, arrow_now, arrow_next, arrow_tip):
    rows, cols = diag_blocks.shape
    pivots = cols // 4
    arrows = arrow_now.shape[0]
    tile = lax.axis_index("tile")
    chip, core = tile // 2, tile % 2
    edge = (chip == 0) | (chip == 3)
    panel_a, panel_c, panel_r = diag_blocks[:, :pivots], coupling[:, :pivots], arrow_now[:, :pivots]
    part = lax.dynamic_slice(arrow_next, (0, tile * rows), (arrows, rows))
    sent_c = jnp.concatenate([panel_c, jnp.concatenate([part[:16], part[16:]], axis=1)], axis=0)
    first, second = [(0, 2), (3, 1), (2, 3), (1, 0)], [(0, 1), (2, 3), (3, 2), (1, 0)]
    third, fourth = [(1, 3), (2, 0)], [(1, 2), (2, 1)]
    near, end = rows // 4, rows * 3 // 4

    e1 = hop(panel_a, first)
    past_c = handed(sent_c)
    o_own = sibling(panel_a)
    e2 = hop(jnp.where(edge, panel_a, e1), second)
    e4 = hop(after(panel_a, e1, past_c, o_own), fourth)
    d1 = handed(after(next_diag[:near], past_c))
    o_e1 = sibling(e1)
    e3 = hop(after(panel_a, e2, e4), third)
    f1 = hop(after(past_c, e2, e4), first)
    d2 = handed(after(next_diag[near:end], e2, d1))
    o_e2 = sibling(after(e2, d1, e4, o_own, o_e1))
    pick = jnp.stack([jnp.where(chip == 0, 0, jnp.where(chip == 2, 1, 2)), core])
    inverse = chain_picked(pick, [panel_a, o_own, e1, o_e1, e2, o_e2])
    solved = nt(jnp.concatenate([panel_a, panel_c, panel_r]), inverse)
    weight = nn(solved, inverse)

    tip = arrow_tip - nt(solved[2 * rows:], solved[2 * rows:])
    tip = jnp.pad(tip.reshape(1, -1), ((0, 7), (0, pivots - arrows * arrows)))
    past_w = handed(jnp.concatenate([weight[rows:], tip]))
    f1, e3, d2 = stage((f1, e3, d2), weight)
    r3 = jnp.where(edge, e3, e4)
    f2 = hop(jnp.where(edge, past_c, f1), second)
    f4 = hop(after(past_c, f1), fourth)
    o_f1, o_r3 = sibling(f1), sibling(r3)

    def spots(*slots):
        return [at for slot in slots for at in (2 * slot + core, 2 * slot + 1 - core)]

    def table(entries):
        return jnp.stack(entries).astype(jnp.int32)

    early = spots(chip, (2 * chip + 1) % 5, 3 * (1 - chip % 2))
    late = spots(2 - chip // 2)
    split = bf16_halves(weight)
    bases = (diag_blocks, coupling, arrow_now)
    at = after(table(early + [tile * rows]), d2, f1, e3)
    out = panel_update(at, split, solved, bases, [panel_a, o_own, e1, o_e1, e2, o_e2], None)
    out = panel_update(table(late + [tile * rows]), split, solved, bases, [r3, o_r3], out)
    past_w, f2, f4 = stage((past_w, f2, f4), out[2])
    f3 = hop(after(past_c, f4, f2), third)
    d3 = handed(after(next_diag[end:], past_w))
    past_tip = past_w[rows + arrows, :arrows * arrows].reshape(arrows, arrows)
    o_f2, o_c = sibling(f2), sibling(after(past_c, f2))
    split = bf16_halves(past_w[:rows + arrows])
    blocks = [past_c, o_c, f1, o_f1, f2, o_f2]
    past_d, past_b = schur_update(table(early), split, [d1, d2], blocks, None)
    d3, f3 = stage((d3, f3), past_b)
    past_d, = schur_update(table(early), split, [d3], blocks, [past_d], rows // near - 1, False)
    s3 = jnp.where(edge, f3, f4)
    gone = schur_update(table(late), split, [d1, d2, d3], [s3, sibling(s3)], [past_d, past_b])
    return (*out, *gone, past_tip)


def local(diag_blocks, coupling, next_diag, arrow_now, arrow_next, arrow_tip):
    rows, cols = diag_blocks.shape
    pivots = cols // 4
    panel_a, panel_c, panel_r = diag_blocks[:, :pivots], coupling[:, :pivots], arrow_now[:, :pivots]
    past_c, past_d, past_b = handed(panel_c), handed(next_diag), handed(arrow_next)
    all_a = lax.all_gather(panel_a, "tile", axis=0, tiled=True)
    inverse = chain(all_a[:pivots])
    solved = nt(jnp.concatenate([panel_a, panel_c, panel_r]), inverse)
    weight = nn(solved, inverse)
    past_w = handed(weight[rows:])
    past_tip = handed(arrow_tip - nt(solved[2 * rows:], solved[2 * rows:]))
    rest = nt(weight, all_a[pivots:])
    row_ids = lax.axis_index("tile") * rows + lax.iota(jnp.int32, rows)
    keep = lax.iota(jnp.int32, cols)[None, :] <= row_ids[:, None]
    factor = jnp.concatenate([solved[:rows], diag_blocks[:, pivots:] - rest[:rows]], axis=1)
    factor = jnp.where(keep, factor, 0.0)
    coupled = jnp.concatenate([solved[rows:2 * rows], coupling[:, pivots:] - rest[rows:2 * rows]], axis=1)
    arrow = jnp.concatenate([solved[2 * rows:], arrow_now[:, pivots:] - rest[2 * rows:]], axis=1)
    all_c = lax.all_gather(past_c, "tile", axis=0, tiled=True)
    past_d = past_d - nt(past_w[:rows], all_c)
    past_b = past_b - nt(past_w[rows:], all_c)
    return (factor, coupled, arrow, past_d, past_b, past_tip)


def solution(mesh):
    split, whole = P(("tm", "tile"), None), P("tm", None)
    return jax.shard_map(
        local_line if mesh.shape["tile"] == 8 else local,
        mesh=mesh,
        in_specs=(split, split, split, whole, whole, whole),
        out_specs=(split, split, whole, split, whole, whole),
        check_vma=False,
    )
```

```python
import functools

import jax
import jax.numpy as jnp
from jax import lax
from jax.experimental import pallas as pl
from jax.experimental.pallas import tpu as pltpu
from jax.sharding import PartitionSpec as P

BLK = 128
precise = lax.Precision.HIGHEST


def dot_nt(a, b):
    return lax.dot_general(a, b, (((1,), (1,)), ((), ())), precision=precise, preferred_element_type=jnp.float32)


def dot_nn(a, b):
    return lax.dot_general(a, b, (((1,), (0,)), ((), ())), precision=precise, preferred_element_type=jnp.float32)


def spread_lane(tile, lane):
    return jnp.broadcast_to(tile[:, lane:lane + 1], (8, BLK))


def spread_row(tile, row):
    return jnp.broadcast_to(tile[row:row + 1, :], (8, BLK))


def diag_inverse(block_ref, inverse_ref):
    groups = BLK // 8
    sub = lax.broadcasted_iota(jnp.int32, (8, BLK), 0)
    lane = lax.broadcasted_iota(jnp.int32, (8, BLK), 1)
    left = [block_ref[8 * g:8 * g + 8, :] for g in range(groups)]
    right = [jnp.where(lane == sub + 8 * g, 1.0, 0.0).astype(jnp.float32) for g in range(groups)]
    for g in range(groups):
        rows, unit = left[g], right[g]
        cols = [spread_lane(rows, 8 * g + c) for c in range(8)]
        scale = jnp.zeros((8, BLK), jnp.float32)
        kept = []
        for k in range(8):
            pivot = spread_row(cols[k], k)
            inv = 1.0 / pivot
            scale = jnp.where(sub == k, lax.rsqrt(pivot), scale)
            row_l, row_r = spread_row(rows, k), spread_row(unit, k)
            heads = {c: spread_row(cols[c], k) for c in range(k + 1, 8)}
            kept.append((inv, row_l, row_r, heads))
            if k < 7:
                f = jnp.where(sub > k, cols[k] * inv, 0.0)
                for c in range(k + 1, 8):
                    cols[c] = cols[c] - f * heads[c]
                rows = rows - f * row_l
                unit = unit - f * row_r
        inverse_ref[8 * g:8 * g + 8, :] = unit * scale
        for r in range(g + 1, groups):
            fac = [spread_lane(left[r], 8 * g + c) for c in range(8)]
            lo, ro = left[r], right[r]
            for k in range(8):
                inv, row_l, row_r, heads = kept[k]
                f = fac[k] * inv
                for c in range(k + 1, 8):
                    fac[c] = fac[c] - f * heads[c]
                lo = lo - f * row_l
                ro = ro - f * row_r
            left[r], right[r] = lo, ro


def chain_kernel(k_ref, out_ref, l_ref, s_ref, g_ref, d_ref, m_ref):
    n = k_ref.shape[0]
    nb = n // BLK
    out_ref[...] = jnp.zeros((n, n), jnp.float32)

    def step(k, carry):
        for i in range(nb):
            @pl.when(k == i)
            def _(i=i):
                at, to = i * BLK, (i + 1) * BLK
                s = k_ref[at:, at:to]
                if i:
                    s = s - dot_nt(l_ref[at:, :at], l_ref[at:to, :at])
                    g_ref[:, :at] = dot_nn(l_ref[at:to, :at], out_ref[:at, :at])
                s_ref[at:, :] = s
                d_ref[...] = s[:BLK]

        diag_inverse(d_ref, m_ref)
        for i in range(nb):
            @pl.when(k == i)
            def _(i=i):
                at, to = i * BLK, (i + 1) * BLK
                m = m_ref[...]
                if i < nb - 1:
                    l_ref[to:, at:to] = dot_nt(s_ref[to:, :], m)
                out_ref[at:to, at:to] = m
                if i:
                    out_ref[at:to, :at] = -dot_nn(m, g_ref[:, :at])
        return carry

    lax.fori_loop(0, nb, step, 0)


def chain(k):
    n = k.shape[0]
    return pl.pallas_call(
        chain_kernel,
        out_shape=jax.ShapeDtypeStruct((n, n), jnp.float32),
        in_specs=[pl.BlockSpec(memory_space=pltpu.VMEM)],
        out_specs=pl.BlockSpec(memory_space=pltpu.VMEM),
        scratch_shapes=[pltpu.VMEM((n, n), jnp.float32), pltpu.VMEM((n, BLK), jnp.float32),
                        pltpu.VMEM((BLK, n), jnp.float32), pltpu.VMEM((BLK, BLK), jnp.float32),
                        pltpu.VMEM((BLK, BLK), jnp.float32)],
        compiler_params=pltpu.CompilerParams(vmem_limit_bytes=40 << 20),
        cost_estimate=pl.CostEstimate(flops=1_000_000, bytes_accessed=1 << 16, transcendentals=0),
    )(k)


def chain_picked_kernel(at_ref, *refs):
    pairs, (out_ref, k_ref, l_ref, s_ref, g_ref, d_ref, m_ref) = refs[:6], refs[6:]
    rows = k_ref.shape[0] // 2
    for which in range(3):
        for core in range(2):
            @pl.when((at_ref[0] == which) & (at_ref[1] == core))
            def _(which=which, core=core):
                pltpu.sync_copy(pairs[2 * which], k_ref.at[core * rows:(core + 1) * rows])
                pltpu.sync_copy(pairs[2 * which + 1], k_ref.at[(1 - core) * rows:(2 - core) * rows])
    chain_kernel(k_ref, out_ref, l_ref, s_ref, g_ref, d_ref, m_ref)


def chain_picked(at, pairs):
    n = 2 * pairs[0].shape[0]
    return pl.pallas_call(
        chain_picked_kernel,
        out_shape=jax.ShapeDtypeStruct((n, n), jnp.float32),
        grid_spec=pltpu.PrefetchScalarGridSpec(
            num_scalar_prefetch=1,
            grid=(1,),
            in_specs=[pl.BlockSpec(memory_space=pl.ANY)] * 6,
            out_specs=pl.BlockSpec((n, n), lambda i, at: (0, 0)),
            scratch_shapes=[pltpu.VMEM((n, n), jnp.float32), pltpu.VMEM((n, n), jnp.float32), pltpu.VMEM((n, BLK), jnp.float32),
                            pltpu.VMEM((BLK, n), jnp.float32), pltpu.VMEM((BLK, BLK), jnp.float32),
                            pltpu.VMEM((BLK, BLK), jnp.float32)],
        ),
        compiler_params=pltpu.CompilerParams(vmem_limit_bytes=40 << 20),
        cost_estimate=pl.CostEstimate(flops=1_000_000, bytes_accessed=1 << 16, transcendentals=0),
    )(at, *pairs)


def halves(x):
    high = x.astype(jnp.bfloat16)
    return high, (x - high.astype(jnp.float32)).astype(jnp.bfloat16)


def product(weights, other):
    (high, low), (other_high, other_low) = weights, other
    dims = (((1,), (1,)), ((), ()))
    total = lax.dot_general(high, other_high, dims, preferred_element_type=jnp.float32)
    total += lax.dot_general(high, other_low, dims, preferred_element_type=jnp.float32)
    return total + lax.dot_general(low, other_high, dims, preferred_element_type=jnp.float32)


LIGHT = pl.CostEstimate(flops=1_000_000, bytes_accessed=1 << 16, transcendentals=0)


def fetch(step, sources, buffer_ref, sems, flag=None):
    count = len(sources) if flag is None else len(sources) // 2

    def run(chosen):
        for i in range(count):
            @pl.when(step == i)
            def _(i=i):
                copies = [pltpu.make_async_copy(chosen[j], buffer_ref.at[j % 2], sems.at[j % 2])
                          for j in (i, i + 1) if j < count]
                if i == 0:
                    copies[0].start()
                if len(copies) > 1:
                    copies[1].start()
                copies[0].wait()

    if flag is None:
        run(sources)
    else:
        pl.when(flag != 0)(lambda: run(sources[:count]))
        pl.when(flag == 0)(lambda: run(sources[count:]))


def panel_update_kernel(count, at_ref, high_ref, low_ref, solved_ref, a_ref, c_ref, r_ref, *rest):
    a_out, c_out, r_out, buffer_ref, sems = rest[-5:]
    step = pl.program_id(0)
    rows = a_ref.shape[0]
    fetch(step, rest[:count], buffer_ref, sems)
    block = at_ref[step]
    keep = (block * rows + lax.broadcasted_iota(jnp.int32, (rows, rows), 1)
            <= at_ref[count] + lax.broadcasted_iota(jnp.int32, (rows, rows), 0))
    solved = block * rows < high_ref.shape[1]

    @pl.when(solved)
    def _():
        a_out[...] = jnp.where(keep, solved_ref[:rows], 0.0)
        c_out[...] = solved_ref[rows:2 * rows]
        r_out[...] = solved_ref[2 * rows:]

    @pl.when(jnp.logical_not(solved))
    def _():
        x = halves(buffer_ref[step % 2])
        a_out[...] = jnp.where(keep, a_ref[...] - product((high_ref[:rows], low_ref[:rows]), x), 0.0)
        c_out[...] = c_ref[...] - product((high_ref[rows:2 * rows], low_ref[rows:2 * rows]), x)
        r_out[...] = r_ref[...] - product((high_ref[2 * rows:], low_ref[2 * rows:]), x)


def panel_update(at, weights, solved, bases, blocks, before):
    rows, arrows, pivots = bases[0].shape[0], bases[2].shape[0], solved.shape[1]
    last = pivots // rows - 1
    count = len(blocks)
    whole = pl.BlockSpec(memory_space=pl.ANY)
    fixed = pl.BlockSpec((2 * rows + arrows, pivots), lambda i, at: (0, 0))
    moving = [pl.BlockSpec((h, rows), lambda i, at: (0, at[i])) for h in (rows, rows, arrows)]
    in_specs = [fixed] * 2 + [pl.BlockSpec((2 * rows + arrows, rows), lambda i, at: (0, jnp.minimum(at[i], last)))]
    in_specs += moving + [whole] * count
    args = [at, *weights, solved, *bases, *blocks]
    aliases = {}
    if before is not None:
        aliases = {len(args) + i: i for i in range(3)}
        in_specs += [whole] * 3
        args += list(before)
    return pl.pallas_call(
        functools.partial(panel_update_kernel, count),
        out_shape=[jax.ShapeDtypeStruct(b.shape, b.dtype) for b in bases],
        grid_spec=pltpu.PrefetchScalarGridSpec(
            num_scalar_prefetch=1, grid=(count,), in_specs=in_specs,
            out_specs=moving,
            scratch_shapes=[pltpu.VMEM((2, rows, pivots), jnp.float32), pltpu.SemaphoreType.DMA((2,))]),
        input_output_aliases=aliases,
        compiler_params=pltpu.CompilerParams(vmem_limit_bytes=48 << 20),
        cost_estimate=LIGHT,
    )(*args)


def schur_update_kernel(count, parts, flagged, at_ref, high_ref, low_ref, *rest):
    bases, sources, (d_out, b_out, buffer_ref, sems) = rest[:parts], rest[parts:parts + count], rest[-4:]
    step = pl.program_id(0)
    height, rows = d_out.shape
    fetch(step, sources, buffer_ref, sems, at_ref[count // 2] if flagged else None)
    x_ref = buffer_ref.at[step % 2]
    x = halves(x_ref[:rows])
    total = product((high_ref[:height], low_ref[:height]), x)
    start = 0
    for base in bases:
        end = start + base.shape[0]
        d_out[start:end] = base[...] - total[start:end]
        start = end
    if start < height:
        d_out[start:] = -total[start:]
    base = jnp.concatenate([x_ref[rows:, :rows], x_ref[rows:, rows:2 * rows]], axis=0)
    b_out[...] = base - product((high_ref[rows:], low_ref[rows:]), x)


def schur_update(at, weights, bases, blocks, before, flagged=False):
    rows, pivots = blocks[0].shape[0] - 16, blocks[0].shape[1]
    arrows, cols = weights[0].shape[0] - rows, bases[0].shape[1]
    count = len(blocks)
    steps = count // 2 if flagged else count
    whole = pl.BlockSpec(memory_space=pl.ANY)
    moving = lambda tall: pl.BlockSpec((tall, rows), lambda i, at: (0, at[i]))
    in_specs = [pl.BlockSpec((rows + arrows, pivots), lambda i, at: (0, 0))] * 2
    in_specs += [moving(base.shape[0]) for base in bases] + [whole] * count
    args = [at, *weights, *bases, *blocks]
    aliases = {}
    if before is not None:
        aliases = {len(args) + i: i for i in range(2)}
        in_specs += [whole] * 2
        args += list(before)
    return pl.pallas_call(
        functools.partial(schur_update_kernel, count, len(bases), flagged),
        out_shape=[jax.ShapeDtypeStruct((rows, cols), jnp.float32), jax.ShapeDtypeStruct((arrows, cols), jnp.float32)],
        grid_spec=pltpu.PrefetchScalarGridSpec(
            num_scalar_prefetch=1, grid=(steps,), in_specs=in_specs, out_specs=[moving(rows), moving(arrows)],
            scratch_shapes=[pltpu.VMEM((2, rows + 16, pivots), jnp.float32), pltpu.SemaphoreType.DMA((2,))]),
        input_output_aliases=aliases,
        compiler_params=pltpu.CompilerParams(vmem_limit_bytes=48 << 20),
        cost_estimate=LIGHT,
    )(*args)


def add_rows_kernel(at_ref, base_ref, before_ref, out_ref):
    out_ref[...] = base_ref[...] + before_ref[...]


def add_rows(at, base, before, width):
    tall = base.shape[0]
    row_at = before.shape[0] // tall - 1
    bottom = pl.BlockSpec((tall, width), lambda i, at: (row_at, at[i]))
    return pl.pallas_call(
        add_rows_kernel,
        out_shape=jax.ShapeDtypeStruct(before.shape, before.dtype),
        grid_spec=pltpu.PrefetchScalarGridSpec(
            num_scalar_prefetch=1, grid=(at.shape[0],),
            in_specs=[pl.BlockSpec((tall, width), lambda i, at: (0, at[i])), bottom], out_specs=bottom),
        input_output_aliases={2: 0},
        cost_estimate=LIGHT,
    )(at, base, before)


def nt(left, right):
    return lax.dot_general(left, right, (((1,), (1,)), ((), ())), precision=lax.Precision.HIGH, preferred_element_type=jnp.float32)


def nn(left, right):
    return lax.dot_general(left, right, (((1,), (0,)), ((), ())), precision=lax.Precision.HIGH, preferred_element_type=jnp.float32)


def handed(value):
    count = lax.axis_size("tm")
    return lax.ppermute(value, "tm", [(t, t + 1) for t in range(count - 1)])


def after(value, *others):
    return lax.optimization_barrier((value,) + others)[0]


def stage(values, *others):
    return lax.optimization_barrier(tuple(values) + others)[:len(values)]


def hop(value, pairs):
    return lax.ppermute(value, "tile", [(2 * a + c, 2 * b + c) for a, b in pairs for c in range(2)])


def sibling(value):
    return lax.ppermute(value, "tile", [(i, i ^ 1) for i in range(8)])


def bf16_halves(x):
    high = lax.reduce_precision(x, 8, 7)
    return high.astype(jnp.bfloat16), (x - high).astype(jnp.bfloat16)


def local_line(diag_blocks, coupling, next_diag, arrow_now, arrow_next, arrow_tip):
    rows, cols = diag_blocks.shape
    pivots = cols // 4
    arrows = arrow_now.shape[0]
    tile = lax.axis_index("tile")
    chip, core = tile // 2, tile % 2
    edge = (chip == 0) | (chip == 3)
    panel_a, panel_c, panel_r = diag_blocks[:, :pivots], coupling[:, :pivots], arrow_now[:, :pivots]
    part = lax.dynamic_slice(arrow_next, (0, tile * rows), (arrows, rows))
    sent_c = jnp.concatenate([panel_c, jnp.concatenate([part[:16], part[16:]], axis=1)], axis=0)
    first, second = [(0, 2), (3, 1), (2, 3), (1, 0)], [(0, 1), (2, 3), (3, 2), (1, 0)]
    third, fourth = [(1, 3), (2, 0)], [(1, 2), (2, 1)]
    near, end = rows // 4, rows * 3 // 4

    e1 = hop(panel_a, first)
    past_c = handed(sent_c)
    o_own = sibling(panel_a)
    e2 = hop(jnp.where(edge, panel_a, e1), second)
    e4 = hop(after(panel_a, e1, o_own), fourth)
    d1 = handed(after(next_diag[:near], past_c))
    o_e1 = sibling(e1)
    e3 = hop(after(panel_a, e2, e4), third)
    f1 = hop(after(past_c, e2, e4), first)
    d2 = handed(after(next_diag[near:end], e2, d1))
    o_e2 = sibling(after(e2, o_own, o_e1))
    pick = jnp.stack([jnp.where(chip == 0, 0, jnp.where(chip == 2, 1, 2)), core])
    inverse = chain_picked(after(pick, d1), [panel_a, o_own, e1, o_e1, e2, o_e2])
    solved = nt(jnp.concatenate([panel_a, panel_c, panel_r]), inverse)
    weight = nn(solved, inverse)

    tip = arrow_tip - nt(solved[2 * rows:], solved[2 * rows:])
    tip = jnp.pad(tip.reshape(1, -1), ((0, 7), (0, pivots - arrows * arrows)))
    past_w = handed(jnp.concatenate([weight[rows:], tip]))
    f1, e3 = stage((f1, e3), weight)
    r3 = jnp.where(edge, e3, e4)
    f2 = hop(jnp.where(edge, past_c, f1), second)
    f4 = hop(after(past_c, f1), fourth)
    o_f1, o_r3 = sibling(f1), sibling(r3)

    def spots(*slots):
        return [at for slot in slots for at in (2 * slot + core, 2 * slot + 1 - core)]

    def table(entries):
        return jnp.stack(entries).astype(jnp.int32)

    early = spots(chip, (2 * chip + 1) % 5, 3 * (1 - chip % 2))
    late = spots(2 - chip // 2)
    split = bf16_halves(weight)
    bases = (diag_blocks, coupling, arrow_now)
    at = after(table(early + [tile * rows]), d2, f1, e3)
    out = panel_update(at, split, solved, bases, [panel_a, o_own, e1, o_e1, e2, o_e2], None)
    out = panel_update(table(late + [tile * rows]), split, solved, bases, [r3, o_r3], out)
    past_w, f2, f4 = stage((past_w, f2, f4), out[2])
    f3 = hop(after(past_c, f4, f2), third)
    d3 = handed(after(next_diag[end:], past_w))
    past_tip = past_w[rows + arrows, :arrows * arrows].reshape(arrows, arrows)
    o_f2, o_f4, o_c = sibling(f2), sibling(f4), sibling(after(past_c, f2))
    split = bf16_halves(past_w[:rows + arrows])
    blocks = [past_c, o_c, f1, o_f1, f2, o_f2]
    past_d, past_b = schur_update(table(early), split, [d1, d2], blocks, None)
    d3, f3 = stage((d3, f3), past_b)
    past_d = add_rows(table(early), d3, past_d, rows)
    blocks = [f3, sibling(f3), f4, o_f4]
    past_d, past_b = schur_update(table(late + [edge]), split, [d1, d2, d3], blocks, [past_d, past_b], True)
    return (*out, past_d, past_b, past_tip)


def local(diag_blocks, coupling, next_diag, arrow_now, arrow_next, arrow_tip):
    rows, cols = diag_blocks.shape
    pivots = cols // 4
    panel_a, panel_c, panel_r = diag_blocks[:, :pivots], coupling[:, :pivots], arrow_now[:, :pivots]
    past_c, past_d, past_b = handed(panel_c), handed(next_diag), handed(arrow_next)
    all_a = lax.all_gather(panel_a, "tile", axis=0, tiled=True)
    inverse = chain(all_a[:pivots])
    solved = nt(jnp.concatenate([panel_a, panel_c, panel_r]), inverse)
    weight = nn(solved, inverse)
    past_w = handed(weight[rows:])
    past_tip = handed(arrow_tip - nt(solved[2 * rows:], solved[2 * rows:]))
    rest = nt(weight, all_a[pivots:])
    row_ids = lax.axis_index("tile") * rows + lax.iota(jnp.int32, rows)
    keep = lax.iota(jnp.int32, cols)[None, :] <= row_ids[:, None]
    factor = jnp.concatenate([solved[:rows], diag_blocks[:, pivots:] - rest[:rows]], axis=1)
    factor = jnp.where(keep, factor, 0.0)
    coupled = jnp.concatenate([solved[rows:2 * rows], coupling[:, pivots:] - rest[rows:2 * rows]], axis=1)
    arrow = jnp.concatenate([solved[2 * rows:], arrow_now[:, pivots:] - rest[2 * rows:]], axis=1)
    all_c = lax.all_gather(past_c, "tile", axis=0, tiled=True)
    past_d = past_d - nt(past_w[:rows], all_c)
    past_b = past_b - nt(past_w[rows:], all_c)
    return (factor, coupled, arrow, past_d, past_b, past_tip)


def solution(mesh):
    split, whole = P(("tm", "tile"), None), P("tm", None)
    return jax.shard_map(
        local_line if mesh.shape["tile"] == 8 else local,
        mesh=mesh,
        in_specs=(split, split, split, whole, whole, whole),
        out_specs=(split, split, whole, split, whole, whole),
        check_vma=False,
    )
```
